128 devices in a mesh: req: 16 (over y, x), tensor: 8 (over z, core).
Axes of the slice: x: 4, y: 4, z: 4, core: 2. Of those that a mesh axis runs over, the one named last changes fastest.
Arguments:
- attn_out: bfloat16 [6144, 2048], P('req', 'tensor'), may hold values from -6 to 6
- w_out: bfloat16 [2048, 2048], P('tensor'), may hold values from -0.125 to 0.125
- residual: bfloat16 [6144, 2048], P('req'), may hold values from -6 to 6
- norm_gain: float32 [2048], replicated, may hold values from 0.5 to 1.5
- expert_ids: int32 [6144, 6], P('req'), may hold values from 0 to 63, all different within a row; in each aligned block of 384 rows (0 to 383, 384 to 767, ...) at most 54 rows name the same one
- gate_weights: bfloat16 [6144, 6], P('req'), may hold values from 0.049804688 to 0.59765625
- w_gate: bfloat16 [128, 2048, 704], P(('req', 'tensor')), may hold values from -0.125 to 0.125
- w_up: bfloat16 [128, 2048, 704], P(('req', 'tensor')), may hold values from -0.125 to 0.125
- w_down: bfloat16 [128, 704, 2048], P(('req', 'tensor')), may hold values from -0.15625 to 0.15625
- s_gate: bfloat16 [2048, 2816], P(None, 'tensor'), may hold values from -0.125 to 0.125
- s_up: bfloat16 [2048, 2816], P(None, 'tensor'), may hold values from -0.125 to 0.125
- s_down: bfloat16 [2816, 2048], P('tensor'), may hold values from -0.109375 to 0.109375
- final_gain: float32 [2048], P('tensor'), may hold values from 0.5 to 1.5
- last_pos: int32 [128], P('req'), may hold values from 0 to 6143, as said below
Outputs:
- hidden_out: bfloat16 [6144, 2048], P('req', 'tensor')
- last_rms: float32 [128], P('req')
- last_peak: float32 [128], P('req')
The draws below stay inside these ranges and needn't reach their ends.
Inputs may be any that keep to these rules, and one draw needn't show every extreme that they name: `expert_ids`: within each device's 384 rows no expert is named by more than 54 of them, a bound that some block reaches; the 6 experts of a row differ. `last_pos`: entry q lies in the rows of index q // 8 of req; entries increase, each such group's last entry is the last of its rows, and the first entry is 0.
All inputs are finite; a program needn't handle non-finite values.
Results may differ from the reference program's by a relative error of at most 0.0065.
Values may be sent and summed in bfloat16 or wider, within the bound.
A program may use at most 192 MiB of HBM per device.

```python
import math
import jax
import jax.numpy as jnp
import numpy as np
from jax import lax

D = 2048
HEADS = 16
HEAD_DIM = 128
FFE = 1408
FFS = 2816
TOP = 6
ROW_DEV = 384
REQ_DEV = 8
EXPERTS = 64
ROWS = 6144
CAP = 54
N_REQ = 16


def draw_last_pos(key, part):
    scores = jax.random.randint(key, (N_REQ, ROW_DEV - 1), 0, 1 << 20)
    scores = scores * ROW_DEV + jnp.arange(ROW_DEV - 1, dtype=jnp.int32)[None, :]
    order = jnp.argsort(scores, axis=1, stable=True).astype(jnp.int32)
    chosen = jnp.sort(order[:, :REQ_DEV - 1], axis=1)
    chosen = chosen.at[0, 0].set(0)
    ending = jnp.full((N_REQ, 1), ROW_DEV - 1, jnp.int32)
    local = jnp.concatenate([chosen, ending], axis=1)
    return (local + ROW_DEV * jnp.arange(N_REQ, dtype=jnp.int32)[:, None]).reshape(-1)


def level_of(own_key, extent, shards, low, largest):
    loudness = 1.0
    for dim, shards_of in shards:
        heights = jax.random.uniform(jax.random.fold_in(jax.random.fold_in(own_key, 6), dim), (shards_of,), jnp.float32, low / len(shards), largest / len(shards))
        loudness = loudness * jnp.repeat(jnp.exp(heights), extent[dim] // shards_of).reshape((-1,) + (1,) * (len(extent) - 1 - dim))
    return loudness


def shared_out(rng, own, number, rows, count, top, bound, slope):
    order = jax.random.permutation(rng, count)
    heavy_load, common = shares(count, rows * top, bound, slope, True), shares(count, rows * top, bound, slope, False)
    places = jnp.arange(count)

    def named(lengths, offset_by):
        used = int((lengths > 0).sum())
        fixed = max(1, used // 4)
        shifted = fixed + (places - fixed + offset_by * (used - fixed)) % max(1, count - fixed)
        return jnp.zeros((count,), jnp.int32).at[order[jnp.where(places < fixed, places, shifted)]].set(jnp.asarray(lengths, jnp.int32))

    lengths = jnp.where(number % 4 == 0, named(heavy_load, number // 4), named(common, number - number // 4 - 1))
    mixed = jax.random.permutation(jax.random.fold_in(own, 3), count)
    donor, taker = mixed[0:count // 2 * 2:2], mixed[1:count // 2 * 2:2]
    margin = jnp.minimum(lengths[donor] - 1, bound - lengths[taker]) // 2
    margin = jnp.where((donor == order[0]) | (taker == order[0]) | (lengths[taker] == 0), 0, jnp.maximum(margin, 0))
    shifted = jax.random.randint(jax.random.fold_in(own, 4), (count // 2,), 0, 1 << 20) % (margin + 1)
    lengths = lengths.at[donor].add(-shifted).at[taker].add(shifted)
    items = jnp.searchsorted(jnp.cumsum(lengths), jnp.arange(rows * top), side="right").astype(jnp.int32)
    grid = items.reshape(top, rows).T
    grid = grid[jax.random.permutation(jax.random.fold_in(own, 1), rows)]
    offset_by = jax.random.randint(jax.random.fold_in(own, 2), (rows, 1), 0, top)
    return jnp.take_along_axis(grid, (jnp.arange(top)[None, :] + offset_by) % top, axis=1)


def shares(number_of, total, reach, slope, full):
    loads = [(1 << 20) // math.isqrt(rank ** slope) + 1 for rank in range(1, number_of + 1)]
    largest = reach if full else min(reach, max(-(-total // number_of), total * loads[0] // sum(loads)))
    least = 1 if total - largest >= number_of - 1 else 0
    counts, spare = [largest] + [least] * (number_of - 1), total - largest - least * (number_of - 1)
    while spare > 0:
        free = [i for i in range(1, number_of) if counts[i] < largest] or [i for i in range(1, number_of) if counts[i] < reach]
        mass, left = sum([loads[i] for i in free]), spare
        for i in free:
            more = min(reach - counts[i], max(1, left * loads[i] // mass), spare)
            counts[i] = counts[i] + more
            spare = spare - more
    return np.array(counts)


def scatter_about(stream_key, shape, deviation, reach, split=(), kind=jnp.bfloat16):
    level = level_of(stream_key, shape, split, -0.22, 0.18) if split else 1.0
    result = jax.random.normal(stream_key, shape, jnp.float32) * deviation * level
    return jnp.minimum(jnp.maximum(result, -reach), reach).astype(kind)


def setup_inputs(seed: int = 0) -> dict:
    arg_keys = jax.random.split(jax.random.key(seed), 15)
    attn_out = scatter_about(arg_keys[0], (ROWS, HEADS * HEAD_DIM), 1.0, 6.0, ((0, 16), (1, 8)))
    w_out = scatter_about(arg_keys[1], (HEADS * HEAD_DIM, D), (HEADS * HEAD_DIM) ** -0.5, 0.125, ((0, 8),))
    residual = scatter_about(arg_keys[2], (ROWS, D), 1.0, 6.0, ((0, 16),))
    norm_gain = jnp.clip(1.0 + 0.1 * jax.random.normal(arg_keys[3], (D,), jnp.float32), 0.5, 1.5)
    expert_ids_keys = jax.random.split(jax.random.fold_in(arg_keys[4], 1), ROWS // ROW_DEV)
    expert_ids_turns = jax.random.permutation(jax.random.fold_in(arg_keys[4], 3), ROWS // ROW_DEV)
    expert_ids = jax.vmap(lambda own, number: shared_out(jax.random.fold_in(arg_keys[4], 2), own, number, ROW_DEV, EXPERTS, TOP, CAP, 2))(expert_ids_keys, expert_ids_turns).reshape((ROWS, TOP))
    gate_weights = jnp.clip(0.049804688 + 0.54785156 * jax.random.uniform(arg_keys[5], (ROWS, TOP), jnp.float32) ** level_of(arg_keys[5], (ROWS, TOP), ((0, 16),), -0.2, 0.2), 0.049804688, 0.59765625).astype(jnp.bfloat16)
    w_gate = scatter_about(arg_keys[6], (2 * EXPERTS, D, FFE // 2), D ** -0.5, 0.125, ((0, 128),))
    w_up = scatter_about(arg_keys[7], (2 * EXPERTS, D, FFE // 2), D ** -0.5, 0.125, ((0, 128),))
    w_down = scatter_about(arg_keys[8], (2 * EXPERTS, FFE // 2, D), FFE ** -0.5, 0.15625, ((0, 128),))
    s_gate = scatter_about(arg_keys[9], (D, FFS), D ** -0.5, 0.125, ((1, 8),))
    s_up = scatter_about(arg_keys[10], (D, FFS), D ** -0.5, 0.125, ((1, 8),))
    s_down = scatter_about(arg_keys[11], (FFS, D), FFS ** -0.5, 0.109375, ((0, 8),))
    final_gain = jnp.clip(1.0 + 0.1 * jax.random.normal(arg_keys[12], (D,), jnp.float32), 0.5, 1.5)
    last_pos = draw_last_pos(jax.random.fold_in(arg_keys[14], 71), 0)
    return {"attn_out": attn_out, "w_out": w_out, "residual": residual, "norm_gain": norm_gain, "expert_ids": expert_ids, "gate_weights": gate_weights, "w_gate": w_gate, "w_up": w_up, "w_down": w_down, "s_gate": s_gate, "s_up": s_up, "s_down": s_down, "final_gain": final_gain, "last_pos": last_pos}


EPSILON = 1e-06

def rms_scale(hidden, gain):
    values = hidden.astype(jnp.float32)
    inverse = lax.rsqrt(lax.optimization_barrier(jnp.mean(values * values, axis=-1, keepdims=True)) + EPSILON)
    return (values * inverse * gain[None, :]).astype(jnp.bfloat16)

def reference(attn_out, w_out, residual, norm_gain, expert_ids, gate_weights, w_gate, w_up, w_down, s_gate, s_up, s_down, final_gain, last_pos):
    hidden = (residual.astype(jnp.float32) + jnp.dot(attn_out, w_out, preferred_element_type=jnp.float32)).astype(jnp.bfloat16)
    normed = rms_scale(hidden, norm_gain)
    shared_act = (jax.nn.silu(jnp.dot(normed, s_gate, preferred_element_type=jnp.float32)) * jnp.dot(normed, s_up, preferred_element_type=jnp.float32)).astype(jnp.bfloat16)
    shared_term = jnp.dot(shared_act, s_down, preferred_element_type=jnp.float32)
    flat_ids = expert_ids.reshape(N_REQ, ROW_DEV * TOP)
    onehot = (flat_ids[:, :, None] == jnp.arange(EXPERTS, dtype=jnp.int32)[None, None, :]).astype(jnp.int32)
    slot_index = lax.optimization_barrier(jnp.sum(jnp.cumsum(onehot, axis=1) * onehot, axis=2)) - 1
    device = jnp.arange(N_REQ, dtype=jnp.int32)[:, None]
    slot_pos = ((flat_ids * N_REQ + device) * CAP + slot_index).reshape(-1).astype(jnp.int32)
    row_ids = (device * ROW_DEV + jnp.arange(ROW_DEV * TOP, dtype=jnp.int32)[None, :] // TOP).reshape(-1).astype(jnp.int32)
    slot_table = jnp.full((EXPERTS * N_REQ * CAP,), ROWS, jnp.int32).at[slot_pos].set(row_ids)
    slot_table = slot_table.reshape(EXPERTS, N_REQ * CAP)
    padded = jnp.concatenate([normed, jnp.zeros((1, D), jnp.bfloat16)], axis=0)
    gate_pairs = w_gate.reshape(EXPERTS, 2, D, FFE // 2)
    up_pairs = w_up.reshape(EXPERTS, 2, D, FFE // 2)
    down_pairs = w_down.reshape(EXPERTS, FFE, D)

    def expert_apply(items):
        table_row, gate_two, up_two, down_mat = items
        gate_mat = jnp.concatenate([gate_two[0], gate_two[1]], axis=1)
        up_mat = jnp.concatenate([up_two[0], up_two[1]], axis=1)
        chosen = padded[table_row]
        gate_proj = jnp.dot(chosen, gate_mat, preferred_element_type=jnp.float32)
        up_proj = jnp.dot(chosen, up_mat, preferred_element_type=jnp.float32)
        activation = (jax.nn.silu(gate_proj) * up_proj).astype(jnp.bfloat16)
        return jnp.dot(activation, down_mat, preferred_element_type=jnp.float32)
    expert_out = lax.map(expert_apply, (slot_table, gate_pairs, up_pairs, down_pairs))
    picked = expert_out.reshape(-1, D)[slot_pos]
    weighted = picked * gate_weights.reshape(-1, 1).astype(jnp.float32)
    routed = lax.optimization_barrier(jnp.sum(weighted.reshape(ROWS, TOP, D), axis=1))
    hidden_out = (hidden.astype(jnp.float32) + shared_term + routed).astype(jnp.bfloat16)
    last_rows = hidden_out[last_pos].astype(jnp.float32)
    last_rms = jnp.sqrt(lax.optimization_barrier(jnp.mean(last_rows * last_rows, axis=1)) + EPSILON)
    last_peak = lax.optimization_barrier(jnp.max(last_rows / last_rms[:, None] * final_gain[None, :], axis=1))
    return (hidden_out, last_rms, last_peak)
```

```python
import functools
import math

import jax
import jax.numpy as jnp
from jax import lax
from jax.experimental import pallas as pl
from jax.experimental.pallas import tpu as pltpu
from jax.sharding import PartitionSpec as P

EPSILON = 1e-06
MESH = pl.DeviceIdType.MESH
BF16 = jnp.bfloat16
F32 = jnp.float32
LANES = 128


def dot(a, b):
    return jnp.dot(a, b, preferred_element_type=F32)


def dot_t(a, b):
    return lax.dot_general(a, b, (((1,), (1,)), ((), ())), preferred_element_type=F32)


def silu(v):
    return v / (1.0 + jnp.exp(-v))


def column_tiles(width, tile):
    return [(start, min(tile, width - start)) for start in range(0, width, tile)]


def layer_kernel(
    dims,
    attn_hbm, wout_hbm, res_hbm, gain_hbm, ids_hbm, gw_hbm, wg_hbm, wu_hbm, wd_hbm,
    sg_hbm, su_hbm, sd_hbm, fgain_hbm, last_hbm,
    out_ref, rms_ref, peak_ref,
    attn_v, wout_v, res_v, ids_v, gw_v, wg_v, wu_v, wd_v, sg_v, su_v, sd_v, gain_ref, fgain_ref, last_ref, load_sem, wout_sem,
    pair_send, pair_recv, part_own, pair_ssem, pair_rsem,
    rs_send, rs_recv, rs_ssem, rs_rsem,
    hid_v, ag_ssem, ag_rsem, sq_col, sq_all, sq_ssem, sq_rsem, inv_v,
    normed_v, nb_ssem, nb_rsem,
    slot_t, pick_v, comb_v,
    disp_v, x_v, dp_ssem, dp_rsem, keep_sem, fw_ssem, fw_rsem,
    act_v, yp_send, yp_recv, y_own, yp_ssem, yp_rsem,
    ret_send, ret_recv, rt_ssem, rt_rsem, local_sem,
    sact_v, sp_send, sp_recv, s_own, sp_ssem, sp_rsem,
    fin_send, fin_recv, fn_ssem, fn_rsem,
    st_all, st_ssem, st_rsem,
):
    NY, NX, NZ, CP = dims["ny"], dims["nx"], dims["nz"], dims["cp"]
    NR, NT = NY * NX, 2 * NZ
    R, D = attn_v.shape[0], wout_v.shape[1]
    FB, DH = D // NT, D // 2
    F, FS, TOP = wg_v.shape[0], sg_v.shape[0], ids_v.shape[0]
    GR = NY * CP
    TN = min(256, DH)
    QD = rms_ref.shape[0]
    ORDER = [0] + sorted(range(1, NZ), key=lambda k: (min(k, NZ - k), k))
    SETS = [(0, 1), (1, NZ)] if NZ < 4 else [(0, 1), (1, 3), (3, NZ)]

    t = lax.axis_index("tensor")
    r = lax.axis_index("req")
    z, c = lax.div(t, 2), lax.rem(t, 2)
    y, x = lax.div(r, NX), lax.rem(r, NX)
    sib = {"tensor": 2 * z + 1 - c}

    def zmod(k):
        return lax.rem(z + k, NZ)

    def zdev(k):
        return {"tensor": 2 * zmod(k) + c}

    def plane(dy, dx):
        return {"req": lax.rem(y + dy, NY) * NX + lax.rem(x + dx, NX)}

    def offset(i):
        dy = lax.rem(i, NY)
        return dy, lax.rem(lax.div(i, NY) + dy, NX)

    def ahead(i):
        return plane(*offset(i))

    def behind(i):
        dy, dx = offset(i)
        return plane(NY - dy, NX - dx)

    def remote(src, dst, ssem, rsem, device):
        return pltpu.make_async_remote_copy(
            src_ref=src, dst_ref=dst, send_sem=ssem, recv_sem=rsem,
            device_id=device, device_id_type=MESH,
        )

    def mul(v, n):
        return pl.multiple_of(v, n)

    def block_cols(kz, core):
        return pl.ds(mul(zmod(kz) * 2 * FB + core * FB, FB), FB)

    def half_cols(j, core, count=1):
        return pl.ds(mul(core * DH + j * FB, FB), count * FB)

    own_half = pl.ds(mul(c * DH, DH), DH)

    barrier = pltpu.get_barrier_semaphore()
    for j in range(1, NT):
        pl.semaphore_signal(barrier, inc=1, device_id={"tensor": lax.rem(t + j, NT)}, device_id_type=MESH)

    @pl.loop(1, NR)
    def _(i):
        pl.semaphore_signal(barrier, inc=1, device_id=ahead(i), device_id_type=MESH)

    loads = [
        pltpu.make_async_copy(src, dst, load_sem.at[n])
        for n, (src, dst) in enumerate([
            (attn_hbm, attn_v), (sd_hbm, sd_v), (ids_hbm, ids_v), (gw_hbm, gw_v),
            (res_hbm.at[:, pl.ds(mul(t * FB, FB), FB)], res_v),
            (gain_hbm, gain_ref), (wd_hbm.at[0], wd_v), (fgain_hbm, fgain_ref), (last_hbm, last_ref),
        ])
    ]
    blocked = [(sg_hbm, sg_v), (su_hbm, su_v), (wg_hbm.at[0], wg_v), (wu_hbm.at[0], wu_v)]
    RS_ORDER = ORDER[::-1]
    weights_in = {}
    loads[0].start()
    for core in (1, 0):
        for kz in RS_ORDER:
            cols = block_cols(kz, c if core == 0 else 1 - c)
            weights_in[core, kz] = pltpu.make_async_copy(
                wout_hbm.at[:, cols], wout_v.at[:, cols], wout_sem.at[core, kz]
            )
            weights_in[core, kz].start()
    for load in loads[2:5]:
        load.start()

    loads[0].wait()
    pair = {}
    for kz in RS_ORDER:
        weights_in[1, kz].wait()
        pair_send[kz] = dot(attn_v[...], wout_v[:, block_cols(kz, 1 - c)]).astype(BF16)
        if not pair:
            pl.semaphore_wait(barrier, NT - 1 + NR - 1)
        pair[kz] = remote(pair_send.at[kz], pair_recv.at[kz], pair_ssem.at[kz], pair_rsem.at[kz], sib)
        pair[kz].start()

    for load in loads[5:] + loads[1:2]:
        load.start()
    for n, (src, dst) in enumerate(blocked):
        for core in range(2):
            for j in range(NZ):
                pltpu.make_async_copy(
                    src.at[:, block_cols(ORDER[j], core)], dst.at[:, half_cols(j, core)], load_sem.at[10 + n]
                ).start()

    def wait_blocked(n):
        src, dst = blocked[n]
        pltpu.make_async_copy(src, dst, load_sem.at[10 + n]).wait()

    for kz in RS_ORDER:
        weights_in[0, kz].wait()
        part_own[kz] = dot(attn_v[...], wout_v[:, block_cols(kz, c)])

    rs = []
    for kz in RS_ORDER[:-1]:
        pair[kz].wait_recv()
        rs_send[kz] = (part_own[kz] + pair_recv[kz].astype(F32)).astype(BF16)
        copy = remote(rs_send.at[kz], rs_recv.at[kz], rs_ssem.at[kz], rs_rsem.at[kz], zdev(kz))
        copy.start()
        rs.append(copy)

    loads[2].wait()
    loads[3].wait()
    place_of = lax.broadcasted_iota(jnp.int32, (NR, R), 0)
    place_dy = place_of & (NY - 1)
    place_dx = ((place_of >> int(math.log2(NY))) + place_dy) & (NX - 1)
    expert_of = ((((y + place_dy) & (NY - 1)) * NX) + ((x + place_dx) & (NX - 1))) * NZ + z
    named = jnp.zeros((NR, R), F32)
    weight = jnp.zeros((NR, R), F32)
    for k in range(TOP):
        hit = ids_v[k:k + 1, :] == expert_of
        named = named + jnp.where(hit, 1.0, 0.0)
        weight = weight + jnp.where(hit, gw_v[k:k + 1, :].astype(F32), 0.0)
    row_of = lax.broadcasted_iota(jnp.int32, (R, R), 0)
    col_of = lax.broadcasted_iota(jnp.int32, (R, R), 1)
    upper = jnp.where(row_of < col_of, 1.0, 0.0).astype(BF16)
    slot = dot(named.astype(BF16), upper)
    slot = jnp.where(named > 0.5, slot, -1.0)
    slot_t[...] = jnp.zeros_like(slot_t)
    slot_t[0:NR, :] = slot
    slot_t[NR:2 * NR, :] = weight
    table = slot_t[...].T.astype(BF16)

    @pl.loop(0, NR // NY)
    def _(g):
        place = lax.broadcasted_iota(jnp.int32, (CP, R), 0).astype(F32)
        parts = []
        for d in range(NY):
            mine = slot_t[pl.ds(g * NY + d, 1), :]
            parts.append(jnp.where(place == mine, 1.0, 0.0))
        pick_v[pl.ds(mul(g * GR, GR), GR), :] = jnp.concatenate(parts, axis=0).astype(BF16)

    for start, width in column_tiles(NR * CP, LANES):
        spot = lax.broadcasted_iota(jnp.int32, (LANES, width), 1) + start
        source = lax.broadcasted_iota(jnp.int32, (LANES, width), 0)
        first = source * CP
        inside = (spot >= first) & (spot < first + CP)
        place = jnp.sum(jnp.where(inside, spot - first, 0).astype(F32), axis=0, keepdims=True)
        slots = dot(table, jnp.where(inside, 1.0, 0.0).astype(BF16))
        first = (source - NR) * CP
        inside = (spot >= first) & (spot < first + CP)
        weights = dot(table, jnp.where(inside, 1.0, 0.0).astype(BF16))
        comb_v[:, start:start + width] = jnp.where(slots == place, weights, 0.0).astype(BF16)

    loads[4].wait()
    pair[0].wait_recv()
    for copy in rs:
        copy.wait_recv()
    step = 64

    @pl.loop(0, R // step)
    def _(m):
        rows = pl.ds(mul(m * step, step), step)
        total = part_own[0, rows, :] + pair_recv[0, rows, :].astype(F32)
        for kz in range(1, NZ):
            total = total + rs_recv[kz, rows, :].astype(F32)
        hid = (res_v[rows, :].astype(F32) + total).astype(BF16)
        hid_v[0, rows, :] = hid
        values = hid.astype(F32)
        sq_col[rows, :] = jnp.broadcast_to(jnp.sum(values * values, axis=-1, keepdims=True), (step, LANES))

    sq_all[0] = sq_col[...].T[0:8, :]
    sq = []
    for j in range(1, NT):
        copy = remote(sq_all.at[0], sq_all.at[j], sq_ssem.at[j], sq_rsem.at[j], {"tensor": lax.rem(t + j, NT)})
        copy.start()
        sq.append(copy)
    ag = [None] * NZ
    for kz in ORDER[1:]:
        j = ORDER.index(NZ - kz)
        ag[j] = remote(hid_v.at[0], hid_v.at[j], ag_ssem.at[j], ag_rsem.at[j], zdev(kz))
        if min(kz, NZ - kz) == 1:
            ag[j].start()
    squares = sq_all[0]
    for j in range(1, NT):
        sq[j - 1].wait_recv()
        squares = squares + sq_all[j]
    inverse = lax.rsqrt(squares / D + EPSILON)
    inv_v[...] = jnp.broadcast_to(inverse[0:1, :], (LANES, R)).T

    nb = []

    def norm_block(j):
        if j:
            ag[j].wait_recv()

        @pl.loop(0, R // step)
        def _(m):
            rows = pl.ds(mul(m * step, step), step)
            scale = jnp.concatenate([inv_v[rows, :]] * (FB // LANES), axis=1)
            normed_v[rows, half_cols(j, c)] = (
                hid_v[j, rows, :].astype(F32) * scale * gain_ref[:, block_cols(ORDER[j], c)]
            ).astype(BF16)

        block = normed_v.at[:, half_cols(j, c)]
        copy = remote(block, block, nb_ssem.at[j], nb_rsem.at[j], sib)
        copy.start()
        nb.append(copy)

    def dispatch_copy(i, s):
        rows = pl.ds(i * CP if isinstance(i, int) else mul(i * CP, 8), CP)
        first, stop = SETS[s]
        return remote(
            disp_v.at[rows, first * FB:stop * FB], x_v.at[rows, half_cols(first, c, stop - first)],
            dp_ssem.at[i, s], dp_rsem.at[i, s], ahead(i),
        )

    first_rows = pl.ds(0, CP)

    def keep_x(s):
        first, stop = SETS[s]
        return pltpu.make_async_copy(
            disp_v.at[first_rows, first * FB:stop * FB], x_v.at[first_rows, half_cols(first, c, stop - first)],
            keep_sem.at[s],
        )

    def dispatch(g, s):
        rows = slice(g * GR, g * GR + GR)
        for j in range(*SETS[s]):
            disp_v[rows, j * FB:(j + 1) * FB] = dot(pick_v[rows, :], normed_v[:, half_cols(j, c)]).astype(BF16)
        for i in range(g * NY, g * NY + NY):
            (dispatch_copy(i, s) if i else keep_x(s)).start()

    loads[5].wait()
    norm_block(0)
    for g in range(NX):
        dispatch(g, 0)
    near = [j for j in range(1, NZ) if min(ORDER[j], NZ - ORDER[j]) == 1]
    far = [j for j in range(1, NZ) if j not in near]
    for j in near:
        ag[j].wait_send()
    for j in far:
        ag[j].start()
    for g in range(NX):
        for s in range(1, len(SETS)):
            if g == 0:
                for j in range(*SETS[s]):
                    norm_block(j)
            dispatch(g, s)

    loads[6].wait()
    wait_blocked(2)
    wait_blocked(3)

    def forward_copy(g, s):
        first, stop = SETS[s]
        block = x_v.at[pl.ds(g * GR if isinstance(g, int) else mul(g * GR, GR), GR), half_cols(first, c, stop - first)]
        return remote(block, block, fw_ssem.at[g, s], fw_rsem.at[g, s], sib)

    def partial_copy(g, kz):
        rows = pl.ds(g * GR if isinstance(g, int) else mul(g * GR, GR), GR)
        return remote(
            yp_send.at[kz, rows, :], yp_recv.at[kz, rows, :], yp_ssem.at[g, kz], yp_rsem.at[g, kz], sib
        )

    def return_copy(i, kz):
        rows = pl.ds(i * CP if isinstance(i, int) else mul(i * CP, 8), CP)
        return remote(
            ret_send.at[kz, rows, :], ret_recv.at[kz, rows, :], rt_ssem.at[i, kz], rt_rsem.at[i, kz], behind(i)
        )

    def keep_y(kz):
        return pltpu.make_async_copy(
            ret_send.at[kz, first_rows, :], ret_recv.at[kz, first_rows, :], local_sem.at[kz]
        )

    z_far = ORDER[:0:-1]
    z_order = z_far + [0]

    def give_back(g, kz):
        rows = slice(g * GR, g * GR + GR)
        partial_copy(g, kz).wait_recv()
        ret_send[kz, rows, :] = (y_own[kz, rows, :] + yp_recv[kz, rows, :].astype(F32)).astype(BF16)
        for i in range(g * NY, g * NY + NY):
            (return_copy(i, kz) if i else keep_y(kz)).start()

    early = NX // 2

    def forward(g, s):
        for i in range(g * NY, g * NY + NY):
            if i:
                dispatch_copy(i, s).wait_recv()
            else:
                keep_x(s).wait()
        forward_copy(g, s).start()

    sets = range(len(SETS))
    for g in range(NX):
        forward(g, 0)
    for s in sets[1:]:
        forward(0, s)
    for g in range(NX):
        rows = slice(g * GR, g * GR + GR)
        for s in sets:
            forward_copy(g, s).wait_recv()
        for start, width in column_tiles(F, TN):
            gate = dot_t(x_v[rows, :], wg_v[start:start + width, :])
            up = dot_t(x_v[rows, :], wu_v[start:start + width, :])
            act_v[:, start:start + width] = (silu(gate) * up).astype(BF16)
        if g + 1 < NX:
            for s in sets[1:]:
                forward(g + 1, s)
        for kz in z_order:
            yp_send[kz, rows, :] = dot(act_v[...], wd_v[:, block_cols(kz, 1 - c)]).astype(BF16)
            partial_copy(g, kz).start()
        for kz in z_order:
            y_own[kz, rows, :] = dot(act_v[...], wd_v[:, block_cols(kz, c)])
        if 0 < g <= early:
            for kz in z_far:
                give_back(g - 1, kz)

    for kz in z_far:
        for g in range(early, NX):
            give_back(g, kz)
    for g in range(NX):
        give_back(g, 0)

    loads[1].wait()
    wait_blocked(0)
    wait_blocked(1)
    for copy in nb:
        copy.wait_recv()

    for start, width in column_tiles(FS, TN):
        gate = dot_t(normed_v[...], sg_v[start:start + width, :])
        up = dot_t(normed_v[...], su_v[start:start + width, :])
        sact_v[:, start:start + width] = (silu(gate) * up).astype(BF16)
    for kz in range(NZ):
        sp_send[kz] = dot(sact_v[...], sd_v[:, block_cols(kz, 1 - c)]).astype(BF16)
    for kz in range(NZ):
        s_own[kz] = dot(sact_v[...], sd_v[:, block_cols(kz, c)])

    shared = remote(sp_send, sp_recv, sp_ssem, sp_rsem, sib)
    shared.start()

    loads[7].wait()
    loads[8].wait()
    q_of = lax.broadcasted_iota(jnp.int32, (QD, R), 0)
    r_of = lax.broadcasted_iota(jnp.int32, (QD, R), 1) + r * R
    chosen = jnp.zeros((QD, R), F32)
    for q in range(QD):
        chosen = jnp.where((q_of == q) & (r_of == last_ref[q]), 1.0, chosen)

    shared.wait_recv()
    fin = []
    for kz in z_order:
        keep_y(kz).wait()

        @pl.loop(1, NR)
        def _(i):
            return_copy(i, kz).wait_recv()

        total = dot(comb_v[...], ret_recv[kz]) + s_own[kz] + sp_recv[kz].astype(F32)
        if not kz:
            s_own[kz] = total
        else:
            fin_send[kz] = total.astype(BF16)
            copy = remote(fin_send.at[kz], fin_recv.at[kz], fn_ssem.at[kz], fn_rsem.at[kz], zdev(kz))
            copy.start()
            fin.append(copy)

    for copy in fin:
        copy.wait_recv()

    total = s_own[0]
    for k in range(1, NZ):
        total = total + fin_recv[k].astype(F32)
    out_ref[...] = (hid_v[0].astype(F32) + total).astype(BF16)

    last = dot(chosen.astype(BF16), out_ref[...])
    squares = jnp.sum(last * last, axis=1, keepdims=True)
    peak = jnp.max(last * fgain_ref[...], axis=1, keepdims=True)
    is_first = lax.broadcasted_iota(jnp.int32, (QD, LANES), 1) == 0
    st_all[0] = jnp.where(is_first, squares, peak)
    st = []
    for j in range(1, NT):
        copy = remote(
            st_all.at[0], st_all.at[j], st_ssem.at[j], st_rsem.at[j], {"tensor": lax.rem(t + j, NT)}
        )
        copy.start()
        st.append(copy)
    squares, peak = st_all[0], st_all[0]
    for j in range(1, NT):
        st[j - 1].wait_recv()
        squares = squares + st_all[j]
        peak = jnp.maximum(peak, st_all[j])
    rms = jnp.sqrt(squares[:, 0:1] / D + EPSILON)
    rms_ref[...] = jnp.broadcast_to(rms, (QD, LANES))
    peak_ref[...] = jnp.broadcast_to(peak[:, 1:2] / rms, (QD, LANES))

    shared.wait_send()
    for copy in list(pair.values()) + rs + sq + [ag[j] for j in far] + nb + fin + st:
        copy.wait_send()

    @pl.loop(1, NR)
    def _(i):
        for s in range(len(SETS)):
            dispatch_copy(i, s).wait_send()
        for kz in range(NZ):
            return_copy(i, kz).wait_send()

    @pl.loop(0, NX)
    def _(g):
        for s in range(len(SETS)):
            forward_copy(g, s).wait_send()
        for kz in range(NZ):
            partial_copy(g, kz).wait_send()


def on_device(
    ny, cap,
    attn_out, w_out, residual, norm_gain, expert_ids, gate_weights, w_gate, w_up, w_down,
    s_gate, s_up, s_down, final_gain, last_pos,
):
    NT, NR = lax.axis_size("tensor"), lax.axis_size("req")
    NZ, NX = NT // 2, NR // ny
    CP = -(-cap // 8) * 8
    R, D = residual.shape
    FB = D // NT
    F, FS, TOP, QD = w_gate.shape[2], s_gate.shape[1], expert_ids.shape[1], last_pos.shape[0]
    SL = NR * CP
    dims = {"ny": ny, "nx": NX, "nz": NZ, "cp": CP}
    dma = pltpu.SemaphoreType.DMA
    vmem = pltpu.VMEM
    scratch = [
        vmem((R, FB), BF16), vmem((FB, D), BF16), vmem((R, FB), BF16), vmem((TOP, R), jnp.int32),
        vmem((TOP, R), BF16), vmem((F, D), BF16), vmem((F, D), BF16), vmem((F, D), BF16),
        vmem((FS, D), BF16), vmem((FS, D), BF16), vmem((FS, D), BF16),
        vmem((1, D), F32), vmem((1, FB), F32), pltpu.SMEM((QD,), jnp.int32), dma((14,)), dma((2, NZ)),
        vmem((NZ, R, FB), BF16), vmem((NZ, R, FB), BF16), vmem((NZ, R, FB), F32), dma((NZ,)), dma((NZ,)),
        vmem((NZ, R, FB), BF16), vmem((NZ, R, FB), BF16), dma((NZ,)), dma((NZ,)),
        vmem((NZ, R, FB), BF16), dma((NZ,)), dma((NZ,)),
        vmem((R, LANES), F32), vmem((NT, 8, R), F32), dma((NT,)), dma((NT,)), vmem((R, LANES), F32),
        vmem((R, D), BF16), dma((NZ,)), dma((NZ,)),
        vmem((LANES, R), F32), vmem((SL, R), BF16), vmem((R, SL), BF16),
        vmem((SL, D // 2), BF16), vmem((SL, D), BF16), dma((NR, 3)), dma((NR, 3)), dma((3,)), dma((NX, 3)), dma((NX, 3)),
        vmem((ny * CP, F), BF16), vmem((NZ, SL, FB), BF16), vmem((NZ, SL, FB), BF16), vmem((NZ, SL, FB), F32),
        dma((NX, NZ)), dma((NX, NZ)),
        vmem((NZ, SL, FB), BF16), vmem((NZ, SL, FB), BF16), dma((NR, NZ)), dma((NR, NZ)), dma((NZ,)),
        vmem((R, FS), BF16), vmem((NZ, R, FB), BF16), vmem((NZ, R, FB), BF16), vmem((NZ, R, FB), F32), dma, dma,
        vmem((NZ, R, FB), BF16), vmem((NZ, R, FB), BF16), dma((NZ,)), dma((NZ,)),
        vmem((NT, QD, LANES), F32), dma((NT,)), dma((NT,)),
    ]
    anywhere = pl.BlockSpec(memory_space=pltpu.HBM)
    inside = pl.BlockSpec(memory_space=pltpu.VMEM)
    hidden_out, last_rms, last_peak = pl.pallas_call(
        functools.partial(layer_kernel, dims),
        name="layer",
        out_shape=(
            pltpu.VMEM((R, FB), BF16),
            pltpu.VMEM((QD, LANES), F32),
            pltpu.VMEM((QD, LANES), F32),
        ),
        in_specs=[anywhere] * 14,
        out_specs=(inside, inside, inside),
        scratch_shapes=scratch,
        compiler_params=pltpu.CompilerParams(
            collective_id=0, has_side_effects=True, vmem_limit_bytes=62_000_000
        ),
    )(
        attn_out, w_out, residual, norm_gain.reshape(1, D), expert_ids.T, gate_weights.T,
        jnp.swapaxes(w_gate, 1, 2), jnp.swapaxes(w_up, 1, 2), w_down, s_gate.T, s_up.T, s_down, final_gain.reshape(1, FB), last_pos,
    )
    return hidden_out, last_rms[:, 0], last_peak[:, 0]


def solution(mesh, ny=4, cap=54):
    return jax.shard_map(
        functools.partial(on_device, ny, cap),
        mesh=mesh,
        in_specs=(
            P("req", "tensor"),
            P("tensor", None),
            P("req", None),
            P(),
            P("req", None),
            P("req", None),
            P(("req", "tensor"), None, None),
            P(("req", "tensor"), None, None),
            P(("req", "tensor"), None, None),
            P(None, "tensor"),
            P(None, "tensor"),
            P("tensor", None),
            P("tensor"),
            P("req"),
        ),
        out_specs=(P("req", "tensor"), P("req"), P("req")),
        check_vma=False,
    )
```

```python
import functools
import math

import jax
import jax.numpy as jnp
from jax import lax
from jax.experimental import pallas as pl
from jax.experimental.pallas import tpu as pltpu
from jax.sharding import PartitionSpec as P

EPSILON = 1e-06
MESH = pl.DeviceIdType.MESH
BF16 = jnp.bfloat16
F32 = jnp.float32
LANES = 128


def dot(a, b):
    return jnp.dot(a, b, preferred_element_type=F32)


def dot_t(a, b):
    return lax.dot_general(a, b, (((1,), (1,)), ((), ())), preferred_element_type=F32)


def silu(v):
    return v / (1.0 + jnp.exp(-v))


def column_tiles(width, tile):
    return [(start, min(tile, width - start)) for start in range(0, width, tile)]


def layer_kernel(
    dims,
    attn_hbm, wout_hbm, res_hbm, gain_hbm, ids_hbm, gw_hbm, wg_hbm, wu_hbm, wd_hbm,
    sg_hbm, su_hbm, sd_hbm, fgain_hbm, last_hbm,
    out_ref, rms_ref, peak_ref,
    attn_v, wout_v, res_v, ids_v, gw_v, wg_v, wu_v, wd_v, sg_v, su_v, sd_v, gain_ref, fgain_ref, last_ref, load_sem, wout_sem,
    pair_send, pair_recv, part_own, pair_ssem, pair_rsem,
    rs_send, rs_recv, rs_ssem, rs_rsem,
    hid_v, ag_ssem, ag_rsem, sq_col, sq_all, sq_ssem, sq_rsem, inv_v,
    normed_v, nb_ssem, nb_rsem,
    slot_t, pick_v, comb_v,
    sc_send, sc_recv, sc_col, sc_ssem, sc_rsem,
    disp_v, x_v, dp_ssem, dp_rsem, keep_sem, fw_ssem, fw_rsem,
    act_v, yp_send, yp_recv, y_own, yp_ssem, yp_rsem,
    ret_send, ret_recv, rt_ssem, rt_rsem, local_sem,
    sact_v, sp_send, sp_recv, s_own, sp_ssem, sp_rsem,
    fin_send, fin_recv, fn_ssem, fn_rsem,
    st_all, st_ssem, st_rsem,
):
    NY, NX, NZ, CP = dims["ny"], dims["nx"], dims["nz"], dims["cp"]
    NR, NT = NY * NX, 2 * NZ
    R, D = attn_v.shape[0], wout_v.shape[1]
    FB, DH = D // NT, D // 2
    F, FS, TOP = wg_v.shape[0], sg_v.shape[0], ids_v.shape[0]
    GR = NY * CP
    TN = min(256, DH)
    QD = rms_ref.shape[0]
    ORDER = [0] + sorted(range(1, NZ), key=lambda k: (min(k, NZ - k), k))
    SETS = [(0, 1), (1, NZ)] if NZ < 4 else [(0, 1), (1, 3), (3, NZ)]

    t = lax.axis_index("tensor")
    r = lax.axis_index("req")
    z, c = lax.div(t, 2), lax.rem(t, 2)
    y, x = lax.div(r, NX), lax.rem(r, NX)
    sib = {"tensor": 2 * z + 1 - c}

    def zmod(k):
        return lax.rem(z + k, NZ)

    def zdev(k):
        return {"tensor": 2 * zmod(k) + c}

    def plane(dy, dx):
        return {"req": lax.rem(y + dy, NY) * NX + lax.rem(x + dx, NX)}

    def offset(i):
        dy = lax.rem(i, NY)
        return dy, lax.rem(lax.div(i, NY) + dy, NX)

    def ahead(i):
        return plane(*offset(i))

    def behind(i):
        dy, dx = offset(i)
        return plane(NY - dy, NX - dx)

    def remote(src, dst, ssem, rsem, device):
        return pltpu.make_async_remote_copy(
            src_ref=src, dst_ref=dst, send_sem=ssem, recv_sem=rsem,
            device_id=device, device_id_type=MESH,
        )

    def mul(v, n):
        return pl.multiple_of(v, n)

    def block_cols(kz, core):
        return pl.ds(mul(zmod(kz) * 2 * FB + core * FB, FB), FB)

    def half_cols(j, core, count=1):
        return pl.ds(mul(core * DH + j * FB, FB), count * FB)

    own_half = pl.ds(mul(c * DH, DH), DH)

    barrier = pltpu.get_barrier_semaphore()
    for j in range(1, NT):
        pl.semaphore_signal(barrier, inc=1, device_id={"tensor": lax.rem(t + j, NT)}, device_id_type=MESH)

    @pl.loop(1, NR)
    def _(i):
        pl.semaphore_signal(barrier, inc=1, device_id=ahead(i), device_id_type=MESH)

    loads = [
        pltpu.make_async_copy(src, dst, load_sem.at[n])
        for n, (src, dst) in enumerate([
            (attn_hbm, attn_v), (sd_hbm, sd_v), (ids_hbm, ids_v), (gw_hbm, gw_v),
            (res_hbm.at[:, pl.ds(mul(t * FB, FB), FB)], res_v),
            (gain_hbm, gain_ref), (wd_hbm.at[0], wd_v), (fgain_hbm, fgain_ref), (last_hbm, last_ref),
        ])
    ]
    blocked = [(sg_hbm, sg_v), (su_hbm, su_v), (wg_hbm.at[0], wg_v), (wu_hbm.at[0], wu_v)]
    RS_ORDER = ORDER[::-1]
    weights_in = {}
    loads[0].start()
    for core in (1, 0):
        for kz in RS_ORDER:
            cols = block_cols(kz, c if core == 0 else 1 - c)
            weights_in[core, kz] = pltpu.make_async_copy(
                wout_hbm.at[:, cols], wout_v.at[:, cols], wout_sem.at[core, kz]
            )
            weights_in[core, kz].start()
    for load in loads[2:5]:
        load.start()

    loads[0].wait()
    pair = {}
    for kz in RS_ORDER:
        weights_in[1, kz].wait()
        pair_send[kz] = dot(attn_v[...], wout_v[:, block_cols(kz, 1 - c)]).astype(BF16)
        if not pair:
            pl.semaphore_wait(barrier, NT - 1 + NR - 1)
        pair[kz] = remote(pair_send.at[kz], pair_recv.at[kz], pair_ssem.at[kz], pair_rsem.at[kz], sib)
        pair[kz].start()

    for load in loads[5:] + loads[1:2]:
        load.start()
    for n, (src, dst) in enumerate(blocked):
        for core in range(2):
            for j in range(NZ):
                pltpu.make_async_copy(
                    src.at[:, block_cols(ORDER[j], core)], dst.at[:, half_cols(j, core)], load_sem.at[10 + n]
                ).start()

    def wait_blocked(n):
        src, dst = blocked[n]
        pltpu.make_async_copy(src, dst, load_sem.at[10 + n]).wait()

    for kz in RS_ORDER:
        weights_in[0, kz].wait()
        part_own[kz] = dot(attn_v[...], wout_v[:, block_cols(kz, c)])

    rs = []
    for kz in RS_ORDER[:-1]:
        pair[kz].wait_recv()
        rs_send[kz] = (part_own[kz] + pair_recv[kz].astype(F32)).astype(BF16)
        copy = remote(rs_send.at[kz], rs_recv.at[kz], rs_ssem.at[kz], rs_rsem.at[kz], zdev(kz))
        copy.start()
        rs.append(copy)

    sc_send[...] = jnp.zeros_like(sc_send)
    loads[2].wait()
    loads[3].wait()
    place_of = lax.broadcasted_iota(jnp.int32, (NR, R), 0)
    place_dy = place_of & (NY - 1)
    place_dx = ((place_of >> int(math.log2(NY))) + place_dy) & (NX - 1)
    expert_of = ((((y + place_dy) & (NY - 1)) * NX) + ((x + place_dx) & (NX - 1))) * NZ + z
    named = jnp.zeros((NR, R), F32)
    weight = jnp.zeros((NR, R), F32)
    for k in range(TOP):
        hit = ids_v[k:k + 1, :] == expert_of
        named = named + jnp.where(hit, 1.0, 0.0)
        weight = weight + jnp.where(hit, gw_v[k:k + 1, :].astype(F32), 0.0)
    row_of = lax.broadcasted_iota(jnp.int32, (R, R), 0)
    col_of = lax.broadcasted_iota(jnp.int32, (R, R), 1)
    upper = jnp.where(row_of < col_of, 1.0, 0.0).astype(BF16)
    slot = dot(named.astype(BF16), upper)
    slot = jnp.where(named > 0.5, slot, -1.0)
    slot_t[...] = jnp.zeros_like(slot_t)
    slot_t[0:NR, :] = slot
    slot_t[NR:2 * NR, :] = weight
    table = slot_t[...].T.astype(BF16)

    @pl.loop(0, NR // NY)
    def _(g):
        place = lax.broadcasted_iota(jnp.int32, (CP, R), 0).astype(F32)
        parts = []
        for d in range(NY):
            mine = slot_t[pl.ds(g * NY + d, 1), :]
            parts.append(jnp.where(place == mine, 1.0, 0.0))
        pick_v[pl.ds(mul(g * GR, GR), GR), :] = jnp.concatenate(parts, axis=0).astype(BF16)

    for start, width in column_tiles(NR * CP, LANES):
        spot = lax.broadcasted_iota(jnp.int32, (LANES, width), 1) + start
        source = lax.broadcasted_iota(jnp.int32, (LANES, width), 0)
        first = source * CP
        inside = (spot >= first) & (spot < first + CP)
        place = jnp.sum(jnp.where(inside, spot - first, 0).astype(F32), axis=0, keepdims=True)
        slots = dot(table, jnp.where(inside, 1.0, 0.0).astype(BF16))
        first = (source - NR) * CP
        inside = (spot >= first) & (spot < first + CP)
        weights = dot(table, jnp.where(inside, 1.0, 0.0).astype(BF16))
        comb_v[:, start:start + width] = jnp.where(slots == place, weights, 0.0).astype(BF16)

    loads[4].wait()
    pair[0].wait_recv()
    for copy in rs:
        copy.wait_recv()
    step = 64

    @pl.loop(0, R // step)
    def _(m):
        rows = pl.ds(mul(m * step, step), step)
        total = part_own[0, rows, :] + pair_recv[0, rows, :].astype(F32)
        for kz in range(1, NZ):
            total = total + rs_recv[kz, rows, :].astype(F32)
        hid = (res_v[rows, :].astype(F32) + total).astype(BF16)
        hid_v[0, rows, :] = hid
        values = hid.astype(F32)
        sq_col[rows, :] = jnp.broadcast_to(jnp.sum(values * values, axis=-1, keepdims=True), (step, LANES))

    sq_all[0] = sq_col[...].T[0:8, :]
    sq = []
    for j in range(1, NT):
        copy = remote(sq_all.at[0], sq_all.at[j], sq_ssem.at[j], sq_rsem.at[j], {"tensor": lax.rem(t + j, NT)})
        copy.start()
        sq.append(copy)
    ag = [None] * NZ
    for kz in ORDER[1:]:
        j = ORDER.index(NZ - kz)
        ag[j] = remote(hid_v.at[0], hid_v.at[j], ag_ssem.at[j], ag_rsem.at[j], zdev(kz))
        if min(kz, NZ - kz) == 1:
            ag[j].start()
    def dispatch_copy(i, s):
        rows = pl.ds(i * CP if isinstance(i, int) else mul(i * CP, 8), CP)
        first, stop = SETS[s]
        return remote(
            disp_v.at[rows, first * FB:stop * FB], x_v.at[rows, half_cols(first, c, stop - first)],
            dp_ssem.at[i, s], dp_rsem.at[i, s], ahead(i),
        )

    first_rows = pl.ds(0, CP)

    def keep_x(s):
        first, stop = SETS[s]
        return pltpu.make_async_copy(
            disp_v.at[first_rows, first * FB:stop * FB], x_v.at[first_rows, half_cols(first, c, stop - first)],
            keep_sem.at[s],
        )

    def dispatch(g, s):
        rows = slice(g * GR, g * GR + GR)
        for j in range(*SETS[s]):
            block = normed_v[:, half_cols(j, c)] if j else hid_v[0]
            disp_v[rows, j * FB:(j + 1) * FB] = dot(pick_v[rows, :], block).astype(BF16)
        for i in range(g * NY, g * NY + NY):
            (dispatch_copy(i, s) if i else keep_x(s)).start()

    for g in range(NX):
        dispatch(g, 0)

    squares = sq_all[0]
    for j in range(1, NT):
        sq[j - 1].wait_recv()
        squares = squares + sq_all[j]
    inverse = lax.rsqrt(squares / D + EPSILON)
    inv_v[...] = jnp.broadcast_to(inverse[0:1, :], (LANES, R)).T

    def scale_copy(i):
        return remote(sc_send.at[i], sc_recv.at[i], sc_ssem.at[i], sc_rsem.at[i], ahead(i))

    keep_scale = pltpu.make_async_copy(sc_send.at[0], sc_recv.at[0], local_sem.at[NZ])
    parts, left = [], inverse[0:1, :]
    for _ in range(3):
        part = left.astype(BF16)
        parts.append(part)
        left = left - part.astype(F32)
    parts = jnp.concatenate(parts + [jnp.zeros((5, R), BF16)], axis=0)
    for i in range(NR):
        slots = dot_t(parts, pick_v[i * CP:(i + 1) * CP, :])
        scale = slots[0:1, :] + slots[1:2, :] + slots[2:3, :]
        sc_send[i, :, 0:CP] = jnp.broadcast_to(scale, (8, CP))
        (scale_copy(i) if i else keep_scale).start()

    nb = []

    def norm_block(j):
        if j:
            ag[j].wait_recv()

        @pl.loop(0, R // step)
        def _(m):
            rows = pl.ds(mul(m * step, step), step)
            scale = jnp.concatenate([inv_v[rows, :]] * (FB // LANES), axis=1)
            normed_v[rows, half_cols(j, c)] = (
                hid_v[j, rows, :].astype(F32) * scale * gain_ref[:, block_cols(ORDER[j], c)]
            ).astype(BF16)

        block = normed_v.at[:, half_cols(j, c)]
        copy = remote(block, block, nb_ssem.at[j], nb_rsem.at[j], sib)
        copy.start()
        nb.append(copy)

    loads[5].wait()
    norm_block(0)
    near = [j for j in range(1, NZ) if min(ORDER[j], NZ - ORDER[j]) == 1]
    far = [j for j in range(1, NZ) if j not in near]
    for j in near:
        ag[j].wait_send()
    for j in far:
        ag[j].start()
    for g in range(NX):
        for s in range(1, len(SETS)):
            if g == 0:
                for j in range(*SETS[s]):
                    norm_block(j)
            dispatch(g, s)

    loads[6].wait()
    wait_blocked(2)
    wait_blocked(3)

    def forward_copy(g, s):
        first, stop = SETS[s]
        block = x_v.at[pl.ds(g * GR if isinstance(g, int) else mul(g * GR, GR), GR), half_cols(first, c, stop - first)]
        return remote(block, block, fw_ssem.at[g, s], fw_rsem.at[g, s], sib)

    def partial_copy(g, kz):
        rows = pl.ds(g * GR if isinstance(g, int) else mul(g * GR, GR), GR)
        return remote(
            yp_send.at[kz, rows, :], yp_recv.at[kz, rows, :], yp_ssem.at[g, kz], yp_rsem.at[g, kz], sib
        )

    def return_copy(i, kz):
        rows = pl.ds(i * CP if isinstance(i, int) else mul(i * CP, 8), CP)
        return remote(
            ret_send.at[kz, rows, :], ret_recv.at[kz, rows, :], rt_ssem.at[i, kz], rt_rsem.at[i, kz], behind(i)
        )

    def keep_y(kz):
        return pltpu.make_async_copy(
            ret_send.at[kz, first_rows, :], ret_recv.at[kz, first_rows, :], local_sem.at[kz]
        )

    z_far = ORDER[:0:-1]
    z_order = z_far + [0]

    def give_back(g, kz):
        rows = slice(g * GR, g * GR + GR)
        partial_copy(g, kz).wait_recv()
        ret_send[kz, rows, :] = (y_own[kz, rows, :] + yp_recv[kz, rows, :].astype(F32)).astype(BF16)
        for i in range(g * NY, g * NY + NY):
            (return_copy(i, kz) if i else keep_y(kz)).start()

    early = NX // 2

    def forward(g, s):
        for i in range(g * NY, g * NY + NY):
            if i:
                dispatch_copy(i, s).wait_recv()
            else:
                keep_x(s).wait()
        if s == 0:
            rows = slice(g * GR, g * GR + GR)
            scale = jnp.concatenate([sc_col[0:CP, 8 * i:8 * i + 1] for i in range(g * NY, g * NY + NY)], axis=0)
            x_v[rows, half_cols(0, c)] = (
                x_v[rows, half_cols(0, c)].astype(F32) * scale * gain_ref[:, block_cols(0, c)]
            ).astype(BF16)
        forward_copy(g, s).start()

    sets = range(len(SETS))
    keep_scale.wait()
    for i in range(1, NR):
        scale_copy(i).wait_recv()
    sc_col[:, 0:8 * NR] = sc_recv[...].reshape(8 * NR, LANES).T
    for g in range(NX):
        forward(g, 0)
    for s in sets[1:]:
        forward(0, s)
    for g in range(NX):
        rows = slice(g * GR, g * GR + GR)
        for s in sets:
            forward_copy(g, s).wait_recv()
        for start, width in column_tiles(F, TN):
            gate = dot_t(x_v[rows, :], wg_v[start:start + width, :])
            up = dot_t(x_v[rows, :], wu_v[start:start + width, :])
            act_v[:, start:start + width] = (silu(gate) * up).astype(BF16)
        if 0 < g <= early:
            for kz in z_far:
                give_back(g - 1, kz)
        if g + 1 < NX:
            for s in sets[1:]:
                forward(g + 1, s)
        for kz in z_order:
            yp_send[kz, rows, :] = dot(act_v[...], wd_v[:, block_cols(kz, 1 - c)]).astype(BF16)
            partial_copy(g, kz).start()
        for kz in z_order:
            y_own[kz, rows, :] = dot(act_v[...], wd_v[:, block_cols(kz, c)])

    for kz in z_far:
        for g in range(early, NX):
            give_back(g, kz)
    for g in range(NX):
        give_back(g, 0)

    loads[1].wait()
    wait_blocked(0)
    wait_blocked(1)
    for copy in nb:
        copy.wait_recv()

    for start, width in column_tiles(FS, TN):
        gate = dot_t(normed_v[...], sg_v[start:start + width, :])
        up = dot_t(normed_v[...], su_v[start:start + width, :])
        sact_v[:, start:start + width] = (silu(gate) * up).astype(BF16)
    for kz in range(NZ):
        sp_send[kz] = dot(sact_v[...], sd_v[:, block_cols(kz, 1 - c)]).astype(BF16)
    for kz in range(NZ):
        s_own[kz] = dot(sact_v[...], sd_v[:, block_cols(kz, c)])

    shared = remote(sp_send, sp_recv, sp_ssem, sp_rsem, sib)
    shared.start()

    loads[7].wait()
    loads[8].wait()
    q_of = lax.broadcasted_iota(jnp.int32, (QD, R), 0)
    r_of = lax.broadcasted_iota(jnp.int32, (QD, R), 1) + r * R
    chosen = jnp.zeros((QD, R), F32)
    for q in range(QD):
        chosen = jnp.where((q_of == q) & (r_of == last_ref[q]), 1.0, chosen)

    shared.wait_recv()
    fin = []
    for kz in z_order:
        keep_y(kz).wait()

        @pl.loop(1, NR)
        def _(i):
            return_copy(i, kz).wait_recv()

        total = dot(comb_v[...], ret_recv[kz]) + s_own[kz] + sp_recv[kz].astype(F32)
        if not kz:
            s_own[kz] = total
        else:
            fin_send[kz] = total.astype(BF16)
            copy = remote(fin_send.at[kz], fin_recv.at[kz], fn_ssem.at[kz], fn_rsem.at[kz], zdev(kz))
            copy.start()
            fin.append(copy)

    for copy in fin:
        copy.wait_recv()

    total = s_own[0]
    for k in range(1, NZ):
        total = total + fin_recv[k].astype(F32)
    out_ref[...] = (hid_v[0].astype(F32) + total).astype(BF16)

    last = dot(chosen.astype(BF16), out_ref[...])
    squares = jnp.sum(last * last, axis=1, keepdims=True)
    peak = jnp.max(last * fgain_ref[...], axis=1, keepdims=True)
    is_first = lax.broadcasted_iota(jnp.int32, (QD, LANES), 1) == 0
    st_all[0] = jnp.where(is_first, squares, peak)
    st = []
    for j in range(1, NT):
        copy = remote(
            st_all.at[0], st_all.at[j], st_ssem.at[j], st_rsem.at[j], {"tensor": lax.rem(t + j, NT)}
        )
        copy.start()
        st.append(copy)
    squares, peak = st_all[0], st_all[0]
    for j in range(1, NT):
        st[j - 1].wait_recv()
        squares = squares + st_all[j]
        peak = jnp.maximum(peak, st_all[j])
    rms = jnp.sqrt(squares[:, 0:1] / D + EPSILON)
    rms_ref[...] = jnp.broadcast_to(rms, (QD, LANES))
    peak_ref[...] = jnp.broadcast_to(peak[:, 1:2] / rms, (QD, LANES))

    shared.wait_send()
    for copy in list(pair.values()) + rs + sq + [ag[j] for j in far] + nb + fin + st:
        copy.wait_send()

    @pl.loop(1, NR)
    def _(i):
        scale_copy(i).wait_send()
        for s in range(len(SETS)):
            dispatch_copy(i, s).wait_send()
        for kz in range(NZ):
            return_copy(i, kz).wait_send()

    @pl.loop(0, NX)
    def _(g):
        for s in range(len(SETS)):
            forward_copy(g, s).wait_send()
        for kz in range(NZ):
            partial_copy(g, kz).wait_send()


def on_device(
    ny, cap,
    attn_out, w_out, residual, norm_gain, expert_ids, gate_weights, w_gate, w_up, w_down,
    s_gate, s_up, s_down, final_gain, last_pos,
):
    NT, NR = lax.axis_size("tensor"), lax.axis_size("req")
    NZ, NX = NT // 2, NR // ny
    CP = -(-cap // 8) * 8
    R, D = residual.shape
    FB = D // NT
    F, FS, TOP, QD = w_gate.shape[2], s_gate.shape[1], expert_ids.shape[1], last_pos.shape[0]
    SL = NR * CP
    dims = {"ny": ny, "nx": NX, "nz": NZ, "cp": CP}
    dma = pltpu.SemaphoreType.DMA
    vmem = pltpu.VMEM
    scratch = [
        vmem((R, FB), BF16), vmem((FB, D), BF16), vmem((R, FB), BF16), vmem((TOP, R), jnp.int32),
        vmem((TOP, R), BF16), vmem((F, D), BF16), vmem((F, D), BF16), vmem((F, D), BF16),
        vmem((FS, D), BF16), vmem((FS, D), BF16), vmem((FS, D), BF16),
        vmem((1, D), F32), vmem((1, FB), F32), pltpu.SMEM((QD,), jnp.int32), dma((14,)), dma((2, NZ)),
        vmem((NZ, R, FB), BF16), vmem((NZ, R, FB), BF16), vmem((NZ, R, FB), F32), dma((NZ,)), dma((NZ,)),
        vmem((NZ, R, FB), BF16), vmem((NZ, R, FB), BF16), dma((NZ,)), dma((NZ,)),
        vmem((NZ, R, FB), BF16), dma((NZ,)), dma((NZ,)),
        vmem((R, LANES), F32), vmem((NT, 8, R), F32), dma((NT,)), dma((NT,)), vmem((R, LANES), F32),
        vmem((R, D), BF16), dma((NZ,)), dma((NZ,)),
        vmem((LANES, R), F32), vmem((SL, R), BF16), vmem((R, SL), BF16),
        vmem((NR, 8, LANES), F32), vmem((NR, 8, LANES), F32), vmem((LANES, LANES), F32), dma((NR,)), dma((NR,)),
        vmem((SL, D // 2), BF16), vmem((SL, D), BF16), dma((NR, 3)), dma((NR, 3)), dma((3,)), dma((NX, 3)), dma((NX, 3)),
        vmem((ny * CP, F), BF16), vmem((NZ, SL, FB), BF16), vmem((NZ, SL, FB), BF16), vmem((NZ, SL, FB), F32),
        dma((NX, NZ)), dma((NX, NZ)),
        vmem((NZ, SL, FB), BF16), vmem((NZ, SL, FB), BF16), dma((NR, NZ)), dma((NR, NZ)), dma((NZ + 1,)),
        vmem((R, FS), BF16), vmem((NZ, R, FB), BF16), vmem((NZ, R, FB), BF16), vmem((NZ, R, FB), F32), dma, dma,
        vmem((NZ, R, FB), BF16), vmem((NZ, R, FB), BF16), dma((NZ,)), dma((NZ,)),
        vmem((NT, QD, LANES), F32), dma((NT,)), dma((NT,)),
    ]
    anywhere = pl.BlockSpec(memory_space=pltpu.HBM)
    inside = pl.BlockSpec(memory_space=pltpu.VMEM)
    hidden_out, last_rms, last_peak = pl.pallas_call(
        functools.partial(layer_kernel, dims),
        name="layer",
        out_shape=(
            pltpu.VMEM((R, FB), BF16),
            pltpu.VMEM((QD, LANES), F32),
            pltpu.VMEM((QD, LANES), F32),
        ),
        in_specs=[anywhere] * 14,
        out_specs=(inside, inside, inside),
        scratch_shapes=scratch,
        compiler_params=pltpu.CompilerParams(
            collective_id=0, has_side_effects=True, vmem_limit_bytes=62_000_000
        ),
    )(
        attn_out, w_out, residual, norm_gain.reshape(1, D), expert_ids.T, gate_weights.T,
        jnp.swapaxes(w_gate, 1, 2), jnp.swapaxes(w_up, 1, 2), w_down, s_gate.T, s_up.T, s_down, final_gain.reshape(1, FB), last_pos,
    )
    return hidden_out, last_rms[:, 0], last_peak[:, 0]


def solution(mesh, ny=4, cap=54):
    return jax.shard_map(
        functools.partial(on_device, ny, cap),
        mesh=mesh,
        in_specs=(
            P("req", "tensor"),
            P("tensor", None),
            P("req", None),
            P(),
            P("req", None),
            P("req", None),
            P(("req", "tensor"), None, None),
            P(("req", "tensor"), None, None),
            P(("req", "tensor"), None, None),
            P(None, "tensor"),
            P(None, "tensor"),
            P("tensor", None),
            P("tensor"),
            P("req"),
        ),
        out_specs=(P("req", "tensor"), P("req"), P("req")),
        check_vma=False,
    )
```

```python
import functools
import math

import jax
import jax.numpy as jnp
from jax import lax
from jax.experimental import pallas as pl
from jax.experimental.pallas import tpu as pltpu
from jax.sharding import PartitionSpec as P

EPSILON = 1e-06
MESH = pl.DeviceIdType.MESH
BF16 = jnp.bfloat16
F32 = jnp.float32
LANES = 128


def dot(a, b):
    return jnp.dot(a, b, preferred_element_type=F32)


def dot_t(a, b):
    return lax.dot_general(a, b, (((1,), (1,)), ((), ())), preferred_element_type=F32)


def silu(v):
    return v / (1.0 + jnp.exp(-v))


def column_tiles(width, tile):
    return [(start, min(tile, width - start)) for start in range(0, width, tile)]


def layer_kernel(
    dims,
    attn_hbm, wout_hbm, res_hbm, gain_hbm, ids_hbm, gw_hbm, wg_hbm, wu_hbm, wd_hbm,
    sg_hbm, su_hbm, sd_hbm, fgain_hbm, last_hbm,
    out_ref, rms_ref, peak_ref,
    attn_v, wout_v, res_v, ids_v, gw_v, wg_v, wu_v, wd_v, sg_v, su_v, sd_v, gain_ref, fgain_ref, last_ref, load_sem, wout_sem,
    pair_send, pair_recv, part_own, pair_ssem, pair_rsem,
    rs_send, rs_recv, rs_ssem, rs_rsem,
    hid_v, ag_ssem, ag_rsem, sq_col, sq_all, sq_ssem, sq_rsem, inv_v,
    normed_v, nb_ssem, nb_rsem,
    slot_t, pick_v, comb_v,
    sc_send, sc_recv, sc_col, sc_ssem, sc_rsem,
    disp_v, x_v, dp_ssem, dp_rsem, keep_sem, fw_ssem, fw_rsem,
    act_v, yp_send, yp_recv, y_own, yp_ssem, yp_rsem,
    ret_send, ret_recv, rt_ssem, rt_rsem, local_sem,
    sact_v, sp_send, sp_recv, s_own, sp_ssem, sp_rsem,
    fin_send, fin_recv, fn_ssem, fn_rsem,
    st_all, st_ssem, st_rsem,
):
    NY, NX, NZ, CP = dims["ny"], dims["nx"], dims["nz"], dims["cp"]
    NR, NT = NY * NX, 2 * NZ
    R, D = attn_v.shape[0], wout_v.shape[1]
    FB, DH = D // NT, D // 2
    F, FS, TOP = wg_v.shape[0], sg_v.shape[0], ids_v.shape[0]
    GR = NY * CP
    TN = min(256, DH)
    QD = rms_ref.shape[0]
    ORDER = [0] + sorted(range(1, NZ), key=lambda k: (min(k, NZ - k), k))
    SETS = [(0, 1), (1, NZ)] if NZ < 4 else [(0, 1), (1, 3), (3, NZ)]

    t = lax.axis_index("tensor")
    r = lax.axis_index("req")
    z, c = lax.div(t, 2), lax.rem(t, 2)
    y, x = lax.div(r, NX), lax.rem(r, NX)
    sib = {"tensor": 2 * z + 1 - c}

    def zmod(k):
        return lax.rem(z + k, NZ)

    def zdev(k):
        return {"tensor": 2 * zmod(k) + c}

    def plane(dy, dx):
        return {"req": lax.rem(y + dy, NY) * NX + lax.rem(x + dx, NX)}

    def offset(i):
        dy = lax.rem(i, NY)
        return dy, lax.rem(lax.div(i, NY) + dy, NX)

    def ahead(i):
        return plane(*offset(i))

    def behind(i):
        dy, dx = offset(i)
        return plane(NY - dy, NX - dx)

    def remote(src, dst, ssem, rsem, device):
        return pltpu.make_async_remote_copy(
            src_ref=src, dst_ref=dst, send_sem=ssem, recv_sem=rsem,
            device_id=device, device_id_type=MESH,
        )

    def mul(v, n):
        return pl.multiple_of(v, n)

    def block_cols(kz, core):
        return pl.ds(mul(zmod(kz) * 2 * FB + core * FB, FB), FB)

    def half_cols(j, core, count=1):
        return pl.ds(mul(core * DH + j * FB, FB), count * FB)

    own_half = pl.ds(mul(c * DH, DH), DH)

    barrier = pltpu.get_barrier_semaphore()
    for j in range(1, NT):
        pl.semaphore_signal(barrier, inc=1, device_id={"tensor": lax.rem(t + j, NT)}, device_id_type=MESH)

    @pl.loop(1, NR)
    def _(i):
        pl.semaphore_signal(barrier, inc=1, device_id=ahead(i), device_id_type=MESH)

    loads = [
        pltpu.make_async_copy(src, dst, load_sem.at[n])
        for n, (src, dst) in enumerate([
            (attn_hbm, attn_v), (sd_hbm, sd_v), (ids_hbm, ids_v), (gw_hbm, gw_v),
            (res_hbm.at[:, pl.ds(mul(t * FB, FB), FB)], res_v),
            (gain_hbm, gain_ref), (wd_hbm.at[0], wd_v), (fgain_hbm, fgain_ref), (last_hbm, last_ref),
        ])
    ]
    blocked = [(sg_hbm, sg_v), (su_hbm, su_v), (wg_hbm.at[0], wg_v), (wu_hbm.at[0], wu_v)]
    RS_ORDER = ORDER[::-1]
    weights_in = {}
    loads[0].start()
    for core in (1, 0):
        for kz in RS_ORDER:
            cols = block_cols(kz, c if core == 0 else 1 - c)
            weights_in[core, kz] = pltpu.make_async_copy(
                wout_hbm.at[:, cols], wout_v.at[:, cols], wout_sem.at[core, kz]
            )
            weights_in[core, kz].start()
    for load in loads[2:5]:
        load.start()

    loads[0].wait()
    pair = {}
    for kz in RS_ORDER:
        weights_in[1, kz].wait()
        pair_send[kz] = dot(attn_v[...], wout_v[:, block_cols(kz, 1 - c)]).astype(BF16)
        if not pair:
            pl.semaphore_wait(barrier, NT - 1 + NR - 1)
        pair[kz] = remote(pair_send.at[kz], pair_recv.at[kz], pair_ssem.at[kz], pair_rsem.at[kz], sib)
        pair[kz].start()

    for load in loads[5:] + loads[1:2]:
        load.start()
    for n, (src, dst) in enumerate(blocked):
        for core in range(2):
            for j in range(NZ):
                pltpu.make_async_copy(
                    src.at[:, block_cols(ORDER[j], core)], dst.at[:, half_cols(j, core)], load_sem.at[10 + n]
                ).start()

    def wait_blocked(n):
        src, dst = blocked[n]
        pltpu.make_async_copy(src, dst, load_sem.at[10 + n]).wait()

    for kz in RS_ORDER:
        weights_in[0, kz].wait()
        part_own[kz] = dot(attn_v[...], wout_v[:, block_cols(kz, c)])

    rs = []
    for kz in RS_ORDER[:-1]:
        pair[kz].wait_recv()
        rs_send[kz] = (part_own[kz] + pair_recv[kz].astype(F32)).astype(BF16)
        copy = remote(rs_send.at[kz], rs_recv.at[kz], rs_ssem.at[kz], rs_rsem.at[kz], zdev(kz))
        copy.start()
        rs.append(copy)

    sc_send[...] = jnp.zeros_like(sc_send)
    loads[2].wait()
    loads[3].wait()
    place_of = lax.broadcasted_iota(jnp.int32, (NR, R), 0)
    place_dy = place_of & (NY - 1)
    place_dx = ((place_of >> int(math.log2(NY))) + place_dy) & (NX - 1)
    expert_of = ((((y + place_dy) & (NY - 1)) * NX) + ((x + place_dx) & (NX - 1))) * NZ + z
    named = jnp.zeros((NR, R), F32)
    weight = jnp.zeros((NR, R), F32)
    for k in range(TOP):
        hit = ids_v[k:k + 1, :] == expert_of
        named = named + jnp.where(hit, 1.0, 0.0)
        weight = weight + jnp.where(hit, gw_v[k:k + 1, :].astype(F32), 0.0)
    row_of = lax.broadcasted_iota(jnp.int32, (R, R), 0)
    col_of = lax.broadcasted_iota(jnp.int32, (R, R), 1)
    upper = jnp.where(row_of < col_of, 1.0, 0.0).astype(BF16)
    slot = dot(named.astype(BF16), upper)
    slot = jnp.where(named > 0.5, slot, -1.0)
    slot_t[...] = jnp.zeros_like(slot_t)
    slot_t[0:NR, :] = slot
    slot_t[NR:2 * NR, :] = weight
    table = slot_t[...].T.astype(BF16)

    @pl.loop(0, NR // NY)
    def _(g):
        place = lax.broadcasted_iota(jnp.int32, (CP, R), 0).astype(F32)
        parts = []
        for d in range(NY):
            mine = slot_t[pl.ds(g * NY + d, 1), :]
            parts.append(jnp.where(place == mine, 1.0, 0.0))
        pick_v[pl.ds(mul(g * GR, GR), GR), :] = jnp.concatenate(parts, axis=0).astype(BF16)

    for start, width in column_tiles(NR * CP, LANES):
        spot = lax.broadcasted_iota(jnp.int32, (LANES, width), 1) + start
        source = lax.broadcasted_iota(jnp.int32, (LANES, width), 0)
        first = source * CP
        inside = (spot >= first) & (spot < first + CP)
        place = jnp.sum(jnp.where(inside, spot - first, 0).astype(F32), axis=0, keepdims=True)
        slots = dot(table, jnp.where(inside, 1.0, 0.0).astype(BF16))
        first = (source - NR) * CP
        inside = (spot >= first) & (spot < first + CP)
        weights = dot(table, jnp.where(inside, 1.0, 0.0).astype(BF16))
        comb_v[:, start:start + width] = jnp.where(slots == place, weights, 0.0).astype(BF16)

    loads[4].wait()
    pair[0].wait_recv()
    for copy in rs:
        copy.wait_recv()
    step = 64

    @pl.loop(0, R // step, unroll=True)
    def _(m):
        rows = pl.ds(mul(m * step, step), step)
        total = part_own[0, rows, :] + pair_recv[0, rows, :].astype(F32)
        for kz in range(1, NZ):
            total = total + rs_recv[kz, rows, :].astype(F32)
        hid = (res_v[rows, :].astype(F32) + total).astype(BF16)
        hid_v[0, rows, :] = hid
        values = hid.astype(F32)
        sq_col[rows, :] = jnp.broadcast_to(jnp.sum(values * values, axis=-1, keepdims=True), (step, LANES))

    sq_all[0] = sq_col[...].T[0:8, :]
    sq = []
    for j in range(1, NT):
        copy = remote(sq_all.at[0], sq_all.at[j], sq_ssem.at[j], sq_rsem.at[j], {"tensor": lax.rem(t + j, NT)})
        copy.start()
        sq.append(copy)
    ag = [None] * NZ
    for kz in ORDER[1:]:
        j = ORDER.index(NZ - kz)
        ag[j] = remote(hid_v.at[0], hid_v.at[j], ag_ssem.at[j], ag_rsem.at[j], zdev(kz))
        if min(kz, NZ - kz) == 1:
            ag[j].start()
    def dispatch_copy(i, s):
        rows = pl.ds(i * CP if isinstance(i, int) else mul(i * CP, 8), CP)
        first, stop = SETS[s]
        return remote(
            disp_v.at[rows, first * FB:stop * FB], x_v.at[rows, half_cols(first, c, stop - first)],
            dp_ssem.at[i, s], dp_rsem.at[i, s], ahead(i),
        )

    first_rows = pl.ds(0, CP)

    def keep_x(s):
        first, stop = SETS[s]
        return pltpu.make_async_copy(
            disp_v.at[first_rows, first * FB:stop * FB], x_v.at[first_rows, half_cols(first, c, stop - first)],
            keep_sem.at[s],
        )

    def dispatch(g, s):
        rows = slice(g * GR, g * GR + GR)
        for j in range(*SETS[s]):
            block = normed_v[:, half_cols(j, c)] if j else hid_v[0]
            disp_v[rows, j * FB:(j + 1) * FB] = dot(pick_v[rows, :], block).astype(BF16)
        for i in range(g * NY, g * NY + NY):
            (dispatch_copy(i, s) if i else keep_x(s)).start()

    for g in range(NX):
        dispatch(g, 0)

    squares = sq_all[0]
    for j in range(1, NT):
        sq[j - 1].wait_recv()
        squares = squares + sq_all[j]
    inverse = lax.rsqrt(squares / D + EPSILON)
    inv_v[...] = jnp.broadcast_to(inverse[0:1, :], (LANES, R)).T

    def scale_copy(i):
        return remote(sc_send.at[i], sc_recv.at[i], sc_ssem.at[i], sc_rsem.at[i], ahead(i))

    keep_scale = pltpu.make_async_copy(sc_send.at[0], sc_recv.at[0], local_sem.at[NZ])
    parts, left = [], inverse[0:1, :]
    for _ in range(3):
        part = left.astype(BF16)
        parts.append(part)
        left = left - part.astype(F32)
    parts = jnp.concatenate(parts + [jnp.zeros((5, R), BF16)], axis=0)
    for i in range(NR):
        slots = dot_t(parts, pick_v[i * CP:(i + 1) * CP, :])
        scale = slots[0:1, :] + slots[1:2, :] + slots[2:3, :]
        sc_send[i, :, 0:CP] = jnp.broadcast_to(scale, (8, CP))
        (scale_copy(i) if i else keep_scale).start()

    nb = []

    def norm_block(j):
        if j:
            ag[j].wait_recv()

        @pl.loop(0, R // step, unroll=True)
        def _(m):
            rows = pl.ds(mul(m * step, step), step)
            scale = jnp.concatenate([inv_v[rows, :]] * (FB // LANES), axis=1)
            normed_v[rows, half_cols(j, c)] = (
                hid_v[j, rows, :].astype(F32) * scale * gain_ref[:, block_cols(ORDER[j], c)]
            ).astype(BF16)

        block = normed_v.at[:, half_cols(j, c)]
        copy = remote(block, block, nb_ssem.at[j], nb_rsem.at[j], sib)
        copy.start()
        nb.append(copy)

    loads[5].wait()
    norm_block(0)
    near = [j for j in range(1, NZ) if min(ORDER[j], NZ - ORDER[j]) == 1]
    far = [j for j in range(1, NZ) if j not in near]
    for j in near:
        ag[j].wait_send()
    for j in far:
        ag[j].start()
    for g in range(NX):
        for s in range(1, len(SETS)):
            if g == 0:
                for j in range(*SETS[s]):
                    norm_block(j)
            dispatch(g, s)

    loads[6].wait()
    wait_blocked(2)
    wait_blocked(3)

    def forward_copy(g, s):
        first, stop = SETS[s]
        block = x_v.at[pl.ds(g * GR if isinstance(g, int) else mul(g * GR, GR), GR), half_cols(first, c, stop - first)]
        return remote(block, block, fw_ssem.at[g, s], fw_rsem.at[g, s], sib)

    def partial_copy(g, kz):
        rows = pl.ds(g * GR if isinstance(g, int) else mul(g * GR, GR), GR)
        return remote(
            yp_send.at[kz, rows, :], yp_recv.at[kz, rows, :], yp_ssem.at[g, kz], yp_rsem.at[g, kz], sib
        )

    def return_copy(i, kz):
        rows = pl.ds(i * CP if isinstance(i, int) else mul(i * CP, 8), CP)
        return remote(
            ret_send.at[kz, rows, :], ret_recv.at[kz, rows, :], rt_ssem.at[i, kz], rt_rsem.at[i, kz], behind(i)
        )

    def keep_y(kz):
        return pltpu.make_async_copy(
            ret_send.at[kz, first_rows, :], ret_recv.at[kz, first_rows, :], local_sem.at[kz]
        )

    z_far = ORDER[:0:-1]
    z_order = z_far + [0]

    def give_back(g, kz):
        rows = slice(g * GR, g * GR + GR)
        partial_copy(g, kz).wait_recv()
        ret_send[kz, rows, :] = (y_own[kz, rows, :] + yp_recv[kz, rows, :].astype(F32)).astype(BF16)
        for i in range(g * NY, g * NY + NY):
            (return_copy(i, kz) if i else keep_y(kz)).start()

    early = NX // 2

    def forward(g, s):
        for i in range(g * NY, g * NY + NY):
            if i:
                dispatch_copy(i, s).wait_recv()
            else:
                keep_x(s).wait()
        if s == 0:
            rows = slice(g * GR, g * GR + GR)
            scale = jnp.concatenate([sc_col[0:CP, 8 * i:8 * i + 1] for i in range(g * NY, g * NY + NY)], axis=0)
            x_v[rows, half_cols(0, c)] = (
                x_v[rows, half_cols(0, c)].astype(F32) * scale * gain_ref[:, block_cols(0, c)]
            ).astype(BF16)
        forward_copy(g, s).start()

    sets = range(len(SETS))
    keep_scale.wait()
    for i in range(1, NR):
        scale_copy(i).wait_recv()
    sc_col[:, 0:8 * NR] = sc_recv[...].reshape(8 * NR, LANES).T
    for g in range(NX):
        forward(g, 0)
    for s in sets[1:]:
        forward(0, s)
    for g in range(NX):
        rows = slice(g * GR, g * GR + GR)
        for s in sets:
            forward_copy(g, s).wait_recv()
        for start, width in column_tiles(F, TN):
            gate = dot_t(x_v[rows, :], wg_v[start:start + width, :])
            up = dot_t(x_v[rows, :], wu_v[start:start + width, :])
            act_v[:, start:start + width] = (silu(gate) * up).astype(BF16)
        if 0 < g <= early:
            for kz in z_far:
                give_back(g - 1, kz)
        if g + 1 < NX:
            for s in sets[1:]:
                forward(g + 1, s)
        for kz in z_order:
            yp_send[kz, rows, :] = dot(act_v[...], wd_v[:, block_cols(kz, 1 - c)]).astype(BF16)
            partial_copy(g, kz).start()
        for kz in z_order:
            y_own[kz, rows, :] = dot(act_v[...], wd_v[:, block_cols(kz, c)])

    for kz in z_far:
        for g in range(early, NX):
            give_back(g, kz)
    for g in range(NX):
        give_back(g, 0)

    loads[1].wait()
    wait_blocked(0)
    wait_blocked(1)
    for copy in nb:
        copy.wait_recv()

    for start, width in column_tiles(FS, TN):
        gate = dot_t(normed_v[...], sg_v[start:start + width, :])
        up = dot_t(normed_v[...], su_v[start:start + width, :])
        sact_v[:, start:start + width] = (silu(gate) * up).astype(BF16)
    for kz in range(NZ):
        sp_send[kz] = dot(sact_v[...], sd_v[:, block_cols(kz, 1 - c)]).astype(BF16)
    for kz in range(NZ):
        s_own[kz] = dot(sact_v[...], sd_v[:, block_cols(kz, c)])

    shared = remote(sp_send, sp_recv, sp_ssem, sp_rsem, sib)
    shared.start()

    loads[7].wait()
    loads[8].wait()
    q_of = lax.broadcasted_iota(jnp.int32, (QD, R), 0)
    r_of = lax.broadcasted_iota(jnp.int32, (QD, R), 1) + r * R
    chosen = jnp.zeros((QD, R), F32)
    for q in range(QD):
        chosen = jnp.where((q_of == q) & (r_of == last_ref[q]), 1.0, chosen)

    shared.wait_recv()
    fin = []
    for kz in z_order:
        keep_y(kz).wait()

        @pl.loop(1, NR)
        def _(i):
            return_copy(i, kz).wait_recv()

        total = dot(comb_v[...], ret_recv[kz]) + s_own[kz] + sp_recv[kz].astype(F32)
        if not kz:
            s_own[kz] = total
        else:
            fin_send[kz] = total.astype(BF16)
            copy = remote(fin_send.at[kz], fin_recv.at[kz], fn_ssem.at[kz], fn_rsem.at[kz], zdev(kz))
            copy.start()
            fin.append(copy)

    for copy in fin:
        copy.wait_recv()

    total = s_own[0]
    for k in range(1, NZ):
        total = total + fin_recv[k].astype(F32)
    out_ref[...] = (hid_v[0].astype(F32) + total).astype(BF16)

    last = dot(chosen.astype(BF16), out_ref[...])
    squares = jnp.sum(last * last, axis=1, keepdims=True)
    peak = jnp.max(last * fgain_ref[...], axis=1, keepdims=True)
    is_first = lax.broadcasted_iota(jnp.int32, (QD, LANES), 1) == 0
    st_all[0] = jnp.where(is_first, squares, peak)
    st = []
    for j in range(1, NT):
        copy = remote(
            st_all.at[0], st_all.at[j], st_ssem.at[j], st_rsem.at[j], {"tensor": lax.rem(t + j, NT)}
        )
        copy.start()
        st.append(copy)
    squares, peak = st_all[0], st_all[0]
    for j in range(1, NT):
        st[j - 1].wait_recv()
        squares = squares + st_all[j]
        peak = jnp.maximum(peak, st_all[j])
    rms = jnp.sqrt(squares[:, 0:1] / D + EPSILON)
    rms_ref[...] = jnp.broadcast_to(rms, (QD, LANES))
    peak_ref[...] = jnp.broadcast_to(peak[:, 1:2] / rms, (QD, LANES))

    shared.wait_send()
    for copy in list(pair.values()) + rs + sq + [ag[j] for j in far] + nb + fin + st:
        copy.wait_send()

    @pl.loop(1, NR)
    def _(i):
        scale_copy(i).wait_send()
        for s in range(len(SETS)):
            dispatch_copy(i, s).wait_send()
        for kz in range(NZ):
            return_copy(i, kz).wait_send()

    @pl.loop(0, NX)
    def _(g):
        for s in range(len(SETS)):
            forward_copy(g, s).wait_send()
        for kz in range(NZ):
            partial_copy(g, kz).wait_send()


def on_device(
    ny, cap,
    attn_out, w_out, residual, norm_gain, expert_ids, gate_weights, w_gate, w_up, w_down,
    s_gate, s_up, s_down, final_gain, last_pos,
):
    NT, NR = lax.axis_size("tensor"), lax.axis_size("req")
    NZ, NX = NT // 2, NR // ny
    CP = -(-cap // 8) * 8
    R, D = residual.shape
    FB = D // NT
    F, FS, TOP, QD = w_gate.shape[2], s_gate.shape[1], expert_ids.shape[1], last_pos.shape[0]
    SL = NR * CP
    dims = {"ny": ny, "nx": NX, "nz": NZ, "cp": CP}
    dma = pltpu.SemaphoreType.DMA
    vmem = pltpu.VMEM
    scratch = [
        vmem((R, FB), BF16), vmem((FB, D), BF16), vmem((R, FB), BF16), vmem((TOP, R), jnp.int32),
        vmem((TOP, R), BF16), vmem((F, D), BF16), vmem((F, D), BF16), vmem((F, D), BF16),
        vmem((FS, D), BF16), vmem((FS, D), BF16), vmem((FS, D), BF16),
        vmem((1, D), F32), vmem((1, FB), F32), pltpu.SMEM((QD,), jnp.int32), dma((14,)), dma((2, NZ)),
        vmem((NZ, R, FB), BF16), vmem((NZ, R, FB), BF16), vmem((NZ, R, FB), F32), dma((NZ,)), dma((NZ,)),
        vmem((NZ, R, FB), BF16), vmem((NZ, R, FB), BF16), dma((NZ,)), dma((NZ,)),
        vmem((NZ, R, FB), BF16), dma((NZ,)), dma((NZ,)),
        vmem((R, LANES), F32), vmem((NT, 8, R), F32), dma((NT,)), dma((NT,)), vmem((R, LANES), F32),
        vmem((R, D), BF16), dma((NZ,)), dma((NZ,)),
        vmem((LANES, R), F32), vmem((SL, R), BF16), vmem((R, SL), BF16),
        vmem((NR, 8, LANES), F32), vmem((NR, 8, LANES), F32), vmem((LANES, LANES), F32), dma((NR,)), dma((NR,)),
        vmem((SL, D // 2), BF16), vmem((SL, D), BF16), dma((NR, 3)), dma((NR, 3)), dma((3,)), dma((NX, 3)), dma((NX, 3)),
        vmem((ny * CP, F), BF16), vmem((NZ, SL, FB), BF16), vmem((NZ, SL, FB), BF16), vmem((NZ, SL, FB), F32),
        dma((NX, NZ)), dma((NX, NZ)),
        vmem((NZ, SL, FB), BF16), vmem((NZ, SL, FB), BF16), dma((NR, NZ)), dma((NR, NZ)), dma((NZ + 1,)),
        vmem((R, FS), BF16), vmem((NZ, R, FB), BF16), vmem((NZ, R, FB), BF16), vmem((NZ, R, FB), F32), dma, dma,
        vmem((NZ, R, FB), BF16), vmem((NZ, R, FB), BF16), dma((NZ,)), dma((NZ,)),
        vmem((NT, QD, LANES), F32), dma((NT,)), dma((NT,)),
    ]
    anywhere = pl.BlockSpec(memory_space=pltpu.HBM)
    inside = pl.BlockSpec(memory_space=pltpu.VMEM)
    hidden_out, last_rms, last_peak = pl.pallas_call(
        functools.partial(layer_kernel, dims),
        name="layer",
        out_shape=(
            pltpu.VMEM((R, FB), BF16),
            pltpu.VMEM((QD, LANES), F32),
            pltpu.VMEM((QD, LANES), F32),
        ),
        in_specs=[anywhere] * 14,
        out_specs=(inside, inside, inside),
        scratch_shapes=scratch,
        compiler_params=pltpu.CompilerParams(
            collective_id=0, has_side_effects=True, vmem_limit_bytes=62_000_000
        ),
    )(
        attn_out, w_out, residual, norm_gain.reshape(1, D), expert_ids.T, gate_weights.T,
        jnp.swapaxes(w_gate, 1, 2), jnp.swapaxes(w_up, 1, 2), w_down, s_gate.T, s_up.T, s_down, final_gain.reshape(1, FB), last_pos,
    )
    return hidden_out, last_rms[:, 0], last_peak[:, 0]


def solution(mesh, ny=4, cap=54):
    return jax.shard_map(
        functools.partial(on_device, ny, cap),
        mesh=mesh,
        in_specs=(
            P("req", "tensor"),
            P("tensor", None),
            P("req", None),
            P(),
            P("req", None),
            P("req", None),
            P(("req", "tensor"), None, None),
            P(("req", "tensor"), None, None),
            P(("req", "tensor"), None, None),
            P(None, "tensor"),
            P(None, "tensor"),
            P("tensor", None),
            P("tensor"),
            P("req"),
        ),
        out_specs=(P("req", "tensor"), P("req"), P("req")),
        check_vma=False,
    )
```
